32 devices in a mesh: shot: 4 (over z), gx: 4 (over x, core), gy: 2 (over y).
Axes of the slice: x: 2, y: 2, z: 4, core: 2. Of those that a mesh axis runs over, the one named last changes fastest.
Arguments:
- partials: float32 [4, 9, 4, 32, 256], P('shot', None, None, 'gx', 'gy'), may hold values from -16 to 16, as said below
- hist_s: float32 [5, 3, 4, 32, 256], P(None, None, 'shot', 'gx', 'gy'), may hold values from -30 to 30
- hist_y: float32 [5, 3, 4, 32, 256], P(None, None, 'shot', 'gx', 'gy'), may hold values from -70 to 70, as said below
Outputs:
- direction: float32 [3, 4, 32, 256], P(None, 'shot', 'gx', 'gy')
The draws below stay inside these ranges and needn't reach their ends.
Inputs may be any that keep to these rules, and one draw needn't show every extreme that they name: `partials`: for every shot group and cell, entries 3, 4, 5 are positive and each exceeds the sum of the magnitudes of the two off-diagonal entries of its row of the 3x3 matrix [[e3, e6, e7], [e6, e4, e8], [e7, e8, e5]]. Each entry of hist_y times the matching entry of hist_s is at least 0.2 times the square of that hist_s entry.
All inputs are finite; a program needn't handle non-finite values.
Results may differ from the reference program's by a relative error of at most 0.00013.
Values sent between devices are 32-bit elements; how exact they have to be, the bound alone decides.
No kernel may reach another device: no remote copies, remote signals or barrier semaphores. Data moves between devices by JAX's collectives and lax.ppermute only.
A program may use at most 64 MiB of HBM per device.

```python
import jax
import jax.numpy as jnp
from jax import lax

PAIRS = 5
NX = 32
NY = 256
NZ = 4
N_SHOT = 4


def common_field(key):
    return jax.random.truncated_normal(jax.random.fold_in(key, 101), -4.0, 4.0, (3, NZ, NX, NY), jnp.float32)


def log_uniform(key, shape, lowest, highest):
    return jnp.exp(jax.random.uniform(key, shape, jnp.float32, jnp.log(lowest), jnp.log(highest)))


def rise_field():
    depth = (jnp.arange(NZ, dtype=jnp.float32) / NZ)[:, None, None]
    across = (jnp.arange(NX, dtype=jnp.float32) / NX)[None, :, None]
    along = (jnp.arange(NY, dtype=jnp.float32) / NY)[None, None, :]
    return jnp.sqrt((1.0 + 2.0 * depth) * (1.0 + 2.0 * across) * (1.0 + 2.0 * along))


def draw_partials(key, part):
    shared = common_field(key)
    grad_scale = log_uniform(jax.random.fold_in(key, 102), (3, NZ, NX, NY), 0.5, 2.0)
    own_part = jax.random.truncated_normal(jax.random.fold_in(key, 103), -4.0, 4.0, (N_SHOT, 3, NZ, NX, NY), jnp.float32)
    gradients = (shared * grad_scale)[None] + 2.0 * own_part
    cell_scale = log_uniform(jax.random.fold_in(key, 104), (NZ, NX, NY), 0.5, 2.0)
    diagonal = jax.random.uniform(jax.random.fold_in(key, 105), (N_SHOT, 3, NZ, NX, NY), jnp.float32, 2.0, 4.0)
    offdiag = jax.random.uniform(jax.random.fold_in(key, 106), (N_SHOT, 3, NZ, NX, NY), jnp.float32, 0.2, 0.9)
    return jnp.concatenate([gradients, cell_scale * diagonal, cell_scale * offdiag], axis=1)


def history_pair(key):
    shared = common_field(key)
    own_part = jax.random.truncated_normal(jax.random.fold_in(key, 201), -4.0, 4.0, (PAIRS, 3, NZ, NX, NY), jnp.float32)
    updates = (0.6 * shared[None] + 0.8 * own_part) * rise_field()
    curvature = log_uniform(jax.random.fold_in(key, 202), (3, NZ, NX, NY), 0.5, 2.0)
    jitter = jax.random.uniform(jax.random.fold_in(key, 203), (PAIRS, 3, NZ, NX, NY), jnp.float32, -1.0, 1.0)
    changes = curvature * updates + 0.3 * jnp.abs(updates) * jitter
    return (updates, changes)


def draw_hist_s(key, part):
    return history_pair(key)[0]


def draw_hist_y(key, part):
    return history_pair(key)[1]


def setup_inputs(seed: int = 0) -> dict:
    key_list = jax.random.split(jax.random.key(seed), 4)
    partials = draw_partials(jax.random.fold_in(key_list[3], 71), 0)
    hist_s = draw_hist_s(jax.random.fold_in(key_list[3], 71), 0)
    hist_y = draw_hist_y(jax.random.fold_in(key_list[3], 71), 0)
    return dict(partials=partials, hist_s=hist_s, hist_y=hist_y)


def smooth_block(padded):
    along_x = 0.25 * (padded[:, :, :-2] + 2.0 * padded[:, :, 1:-1] + padded[:, :, 2:])
    return 0.25 * (along_x[..., :-2] + 2.0 * along_x[..., 1:-1] + along_x[..., 2:])


def apply_inverse(hessian, vectors):
    diag_p = hessian[0]
    diag_s = hessian[1]
    diag_r = hessian[2]
    cross_ps = hessian[3]
    cross_pr = hessian[4]
    cross_sr = hessian[5]
    cof_pp = diag_s * diag_r - cross_sr * cross_sr
    cof_ps = cross_pr * cross_sr - cross_ps * diag_r
    cof_pr = cross_ps * cross_sr - diag_s * cross_pr
    cof_ss = diag_p * diag_r - cross_pr * cross_pr
    cof_sr = cross_ps * cross_pr - diag_p * cross_sr
    cof_rr = diag_p * diag_s - cross_ps * cross_ps
    determinant = diag_p * cof_pp + cross_ps * cof_ps + cross_pr * cof_pr
    inverse_det = 1.0 / determinant
    comp_one = vectors[:, 0]
    comp_two = vectors[:, 1]
    comp_three = vectors[:, 2]
    return jnp.stack([
        (cof_pp * comp_one + cof_ps * comp_two + cof_pr * comp_three) * inverse_det,
        (cof_ps * comp_one + cof_ss * comp_two + cof_sr * comp_three) * inverse_det,
        (cof_pr * comp_one + cof_sr * comp_two + cof_rr * comp_three) * inverse_det], axis=1)


def pair_dots(left_flat, right_flat):
    return lax.dot_general(left_flat, right_flat, (((1,), (1,)), ((), ())),
                           precision=lax.Precision.HIGHEST, preferred_element_type=jnp.float32)


def upper_solve(matrix, values):
    count = matrix.shape[0]
    found = [None] * count
    for row in range(count - 1, -1, -1):
        total = values[row]
        for col in range(row + 1, count):
            total = total - matrix[row, col] * found[col]
        found[row] = total / matrix[row, row]
    return jnp.stack(found)


def upper_transpose_solve(matrix, values):
    count = matrix.shape[0]
    found = [None] * count
    for row in range(count):
        total = values[row]
        for col in range(row):
            total = total - matrix[col, row] * found[col]
        found[row] = total / matrix[row, row]
    return jnp.stack(found)


def combine_terms(cross_gram, curv_gram, hist_dot, pre_dot, solved, hist_s):
    middle_part = jnp.diag(jnp.diag(cross_gram)) + curv_gram
    coef_p = upper_solve(cross_gram, hist_dot)
    right_hand = jnp.dot(middle_part, coef_p, precision=lax.Precision.HIGHEST) - pre_dot
    coef_q = upper_transpose_solve(cross_gram, right_hand)
    update_s = jnp.tensordot(coef_q, hist_s, axes=1, precision=lax.Precision.HIGHEST)
    update_z = jnp.tensordot(coef_p, solved[1:], axes=1, precision=lax.Precision.HIGHEST)
    return -(solved[0] + update_s - update_z)


def reference(partials, hist_s, hist_y):
    fields = jnp.sum(partials, axis=0) * (1.0 / N_SHOT)
    padded = jnp.pad(fields, ((0, 0), (0, 0), (1, 1), (1, 1)))
    smoothed = smooth_block(padded)
    gradient = smoothed[0:3]
    solved = apply_inverse(smoothed[3:9], jnp.concatenate([gradient[None], hist_y], axis=0))
    s_flat = hist_s.reshape(PAIRS, -1)
    y_flat = hist_y.reshape(PAIRS, -1)
    z_flat = solved[1:].reshape(PAIRS, -1)
    cross_gram = pair_dots(s_flat, y_flat)
    curv_gram = pair_dots(y_flat, z_flat)
    hist_dot = pair_dots(s_flat, gradient.reshape(1, -1))[:, 0]
    pre_dot = pair_dots(y_flat, solved[0].reshape(1, -1))[:, 0]
    return combine_terms(cross_gram, curv_gram, hist_dot, pre_dot, solved, hist_s)
```

```python
import functools

import jax
import jax.numpy as jnp
from jax import lax
from jax.experimental import pallas as pl
from jax.experimental.pallas import tpu as pltpu
from jax.sharding import PartitionSpec as P

PAIRS = 5
FIELDS = 9
AXES = ("shot", "gx", "gy")
TRI = [(i, j) for i in range(PAIRS) for j in range(i, PAIRS)]
SLOTS = 2 * len(TRI) + 2 * PAIRS
GROUPS = -(-SLOTS // 8)


VMEM = pl.BlockSpec(memory_space=pltpu.VMEM)


def call(kernel, out_shapes, args, scratch=()):
    out = [jax.ShapeDtypeStruct(shape, jnp.float32) for shape in out_shapes]
    return pl.pallas_call(
        kernel,
        out_shape=out,
        in_specs=[VMEM] * len(args),
        out_specs=[VMEM] * len(out),
        scratch_shapes=[pltpu.VMEM(shape, jnp.float32) for shape in scratch],
    )(*args)


def power_of_two(n):
    return n & (n - 1) == 0


def lanes(shape):
    return lax.broadcasted_iota(jnp.int32, shape, len(shape) - 1)


def sum_kernel(scale, ends, count, *refs):
    blocks, fields_ref, cols = refs[:count], refs[count], refs[count + 1 :]
    levels, rows, width = fields_ref.shape[1:]
    lane = lanes((rows, width))
    for level in range(levels):
        packed = [jnp.zeros((rows, width), jnp.float32) for _ in cols]
        for f in range(FIELDS):
            total = blocks[0][f, level]
            for block in blocks[1:]:
                total = total + block[f, level]
            total = total * scale
            fields_ref[f, level] = total
            for k, end in enumerate(ends()):
                moved = pltpu.roll(total, (f + width - end) % width, 1)
                packed[k] = jnp.where(lane == f, moved, packed[k])
        for k, col in enumerate(cols):
            col[level] = packed[k]


def along_y_kernel(slots, fields_ref, *refs):
    received, (out_ref, first_ref, last_ref) = refs[:-3], refs[-3:]
    levels, rows, width = fields_ref.shape[1:]
    lane = lanes((rows, width))
    targets = slots()
    for level in range(levels):
        for f in range(FIELDS):
            own = fields_ref[f, level]
            left = jnp.where(lane == 0, 0.0, pltpu.roll(own, 1, 1))
            right = jnp.where(lane == width - 1, 0.0, pltpu.roll(own, width - 1, 1))
            for ref, (target, valid) in zip(received, targets):
                moved = pltpu.roll(ref[level], (target + width - f) % width, 1)
                hit = lane == target
                if valid is not None:
                    hit = jnp.logical_and(hit, valid)
                left = left + jnp.where(hit, moved, 0.0)
            value = 0.25 * (left + 2.0 * own + right)
            out_ref[f, level] = value
            first_ref[level, f : f + 1] = value[0:1]
            last_ref[level, f : f + 1] = value[rows - 1 : rows]


def dots_kernel(filtered_ref, above_ref, below_ref, s_ref, y_ref, solved_ref, part_ref, slot_ref):
    levels, rows, width = filtered_ref.shape[1:]
    sub = lax.broadcasted_iota(jnp.int32, (rows, width), 0)
    at = lax.axis_index("gx")
    has_above = jnp.where(at > 0, 1.0, 0.0)
    has_below = jnp.where(at < lax.axis_size("gx") - 1, 1.0, 0.0)
    sums = [None] * SLOTS

    def add(slot, value):
        sums[slot] = value if sums[slot] is None else sums[slot] + value

    for level in range(levels):
        smooth = []
        for f in range(FIELDS):
            own = filtered_ref[f, level]
            above = jnp.broadcast_to(above_ref[level, f : f + 1] * has_above, own.shape)
            below = jnp.broadcast_to(below_ref[level, f : f + 1] * has_below, own.shape)
            up = jnp.where(sub == 0, above, pltpu.roll(own, 1, 0))
            down = jnp.where(sub == rows - 1, below, pltpu.roll(own, rows - 1, 0))
            smooth.append(0.25 * (up + 2.0 * own + down))
        grad = smooth[0:3]
        diag_p, diag_s, diag_r, cross_ps, cross_pr, cross_sr = smooth[3:9]
        cof_pp = diag_s * diag_r - cross_sr * cross_sr
        cof_ps = cross_pr * cross_sr - cross_ps * diag_r
        cof_pr = cross_ps * cross_sr - diag_s * cross_pr
        cof_ss = diag_p * diag_r - cross_pr * cross_pr
        cof_sr = cross_ps * cross_pr - diag_p * cross_sr
        cof_rr = diag_p * diag_s - cross_ps * cross_ps
        determinant = diag_p * cof_pp + cross_ps * cof_ps + cross_pr * cof_pr
        inverse_det = 1.0 / determinant

        def solve(vec):
            one, two, three = vec
            return [
                (cof_pp * one + cof_ps * two + cof_pr * three) * inverse_det,
                (cof_ps * one + cof_ss * two + cof_sr * three) * inverse_det,
                (cof_pr * one + cof_sr * two + cof_rr * three) * inverse_det,
            ]

        def dot(a, b):
            return a[0] * b[0] + a[1] * b[1] + a[2] * b[2]

        s = [[s_ref[i, p, level] for p in range(3)] for i in range(PAIRS)]
        y = [[y_ref[i, p, level] for p in range(3)] for i in range(PAIRS)]
        newton = solve(grad)
        for p in range(3):
            solved_ref[0, p, level] = newton[p]
        for j in range(PAIRS):
            z = solve(y[j])
            for p in range(3):
                solved_ref[1 + j, p, level] = z[p]
            for i in range(j + 1):
                add(TRI.index((i, j)), dot(s[i], y[j]))
                add(len(TRI) + TRI.index((i, j)), dot(y[i], z))
            add(2 * len(TRI) + j, dot(s[j], grad))
            add(2 * len(TRI) + PAIRS + j, dot(y[j], newton))

    for slot in range(8 * GROUPS):
        value = sums[slot] if slot < SLOTS else jnp.zeros((rows, width), jnp.float32)
        slot_ref[slot * rows : (slot + 1) * rows] = value
    lane = lanes((8, width))
    packed = jnp.zeros((8, width), jnp.float32)
    for group in range(GROUPS):
        total = None
        for r in range(rows):
            piece = slot_ref[pl.ds(group * 8 * rows + r, 8, stride=rows)]
            total = piece if total is None else total + piece
        packed = jnp.where(lane == group, jnp.sum(total, axis=1, keepdims=True), packed)
    part_ref[...] = packed


def combine_kernel(count, *refs):
    parts, (solved_ref, s_ref, out_ref, spread_ref) = refs[:count], refs[count:]
    levels, rows, width = s_ref.shape[2:]
    packed = parts[0][...]
    for part in parts[1:]:
        packed = packed + part[...]
    for group in range(GROUPS):
        spread_ref[group * 8 : (group + 1) * 8] = jnp.broadcast_to(
            packed[:, group : group + 1], (8, width)
        )

    def entry(slot):
        return spread_ref[slot : slot + 1]

    cross = {pair: entry(k) for k, pair in enumerate(TRI)}
    curv = {pair: entry(len(TRI) + k) for k, pair in enumerate(TRI)}
    hist_dot = [entry(2 * len(TRI) + i) for i in range(PAIRS)]
    pre_dot = [entry(2 * len(TRI) + PAIRS + i) for i in range(PAIRS)]
    inverse = [1.0 / cross[i, i] for i in range(PAIRS)]
    coef_p = [None] * PAIRS
    for row in range(PAIRS - 1, -1, -1):
        total = hist_dot[row]
        for col in range(PAIRS - 1, row, -1):
            total = total - cross[row, col] * coef_p[col]
        coef_p[row] = total * inverse[row]
    coef_q = [None] * PAIRS
    for row in range(PAIRS):
        total = cross[row, row] * coef_p[row] - pre_dot[row]
        for col in range(PAIRS):
            total = total + curv[min(row, col), max(row, col)] * coef_p[col]
        for col in range(row):
            total = total - cross[col, row] * coef_q[col]
        coef_q[row] = total * inverse[row]
    coef_p = [jnp.broadcast_to(c, (rows, width)) for c in coef_p]
    coef_q = [jnp.broadcast_to(c, (rows, width)) for c in coef_q]
    for p in range(3):
        for level in range(levels):
            total = solved_ref[0, p, level]
            for i in range(PAIRS):
                total = total + coef_q[i] * s_ref[i, p, level]
                total = total - coef_p[i] * solved_ref[1 + i, p, level]
            out_ref[p, level] = -total


def shifted(x, axis, step):
    n = lax.axis_size(axis)
    return lax.ppermute(x, axis, [(i, (i + step) % n) for i in range(n)])


def flipped(x, flips):
    sizes = [lax.axis_size(a) for a in AXES]
    pairs = []
    for i in range(sizes[0]):
        for j in range(sizes[1]):
            for k in range(sizes[2]):
                to = [a ^ flips.get(n, 0) for n, a in zip(AXES, (i, j, k))]
                pairs.append(
                    (
                        (i * sizes[1] + j) * sizes[2] + k,
                        (to[0] * sizes[1] + to[1]) * sizes[2] + to[2],
                    )
                )
    return lax.ppermute(x, AXES, pairs)


def shot_blocks(partials):
    n = lax.axis_size("shot")
    levels = partials.shape[1] // n
    if n > 8 or not power_of_two(n):
        return [lax.psum_scatter(partials, "shot", scatter_dimension=1, tiled=True)]
    me = lax.axis_index("shot")

    def block(k):
        return lax.dynamic_slice_in_dim(partials, (me ^ k) * levels, levels, axis=1)

    blocks = [block(0)]
    for k in range(n - 1, 0, -1):
        blocks.append(flipped(block(k), {"shot": k}))
    return blocks


def all_sums(part):
    if not all(power_of_two(lax.axis_size(a)) for a in AXES):
        return [lax.psum(part, AXES)]
    bits = {a: [1 << b for b in range(lax.axis_size(a).bit_length() - 1)] for a in AXES}
    stages = []
    for bit in bits["shot"][:0:-1]:
        stages.append([{"shot": bit}])
    last = bits["shot"][:1]
    flips = [{"gy": m} for m in bits["gy"][:1]] + [{"shot": m} for m in last]
    if len(flips) == 2:
        flips.append({**flips[0], **flips[1]})
    stages.append(flips)
    for bit in bits["gy"][1:]:
        stages.append([{"gy": bit}])
    stages.append([{"gx": m} for m in range(1, lax.axis_size("gx"))])
    pieces = [part]
    for stage in stages:
        if not stage:
            continue
        part = functools.reduce(jnp.add, pieces)
        pieces = [part] + [flipped(part, flip) for flip in stage]
    return pieces


def per_device(partials, hist_s, hist_y):
    levels, rows, width = hist_s.shape[2:]
    blocks = shot_blocks(partials[0])
    scale = 1.0 / lax.axis_size("shot")
    n_y = lax.axis_size("gy")
    tile = (FIELDS, levels, rows, width)
    col = (levels, rows, width)

    if n_y == 2:
        def ends():
            return [jnp.where(lax.axis_index("gy") == 0, width - 1, 0)]

        def slots():
            return [(jnp.where(lax.axis_index("gy") == 0, width - 1, 0), None)]
    else:

        def ends():
            return [0, width - 1]

        def slots():
            at = lax.axis_index("gy")
            return [(width - 1, at < n_y - 1), (0, at > 0)]

    sends = 1 if n_y == 2 else 2
    fields, *cols = call(
        functools.partial(sum_kernel, scale, ends, len(blocks)), [tile] + [col] * sends, blocks
    )
    if n_y == 2:
        received = [shifted(cols[0], "gy", 1)]
    else:
        received = [shifted(cols[0], "gy", -1), shifted(cols[1], "gy", 1)]
    edge = (levels, FIELDS, width)
    filtered, first, last = call(
        functools.partial(along_y_kernel, slots), [tile, edge, edge], [fields] + received
    )
    above = shifted(last, "gx", 1)
    below = shifted(first, "gx", -1)
    solved, part = call(
        dots_kernel,
        [(1 + PAIRS, 3, levels, rows, width), (8, width)],
        [filtered, above, below, hist_s, hist_y],
        [(8 * GROUPS * rows, width)],
    )
    pieces = all_sums(part)
    (direction,) = call(
        functools.partial(combine_kernel, len(pieces)),
        [(3, levels, rows, width)],
        pieces + [solved, hist_s],
        [(8 * GROUPS, width)],
    )
    return direction


def solution(mesh):
    return jax.shard_map(
        per_device,
        mesh=mesh,
        in_specs=(
            P("shot", None, None, "gx", "gy"),
            P(None, None, "shot", "gx", "gy"),
            P(None, None, "shot", "gx", "gy"),
        ),
        out_specs=P(None, "shot", "gx", "gy"),
        check_vma=False,
    )
```

```python
import functools

import jax
import jax.numpy as jnp
from jax import lax
from jax.experimental import pallas as pl
from jax.experimental.pallas import tpu as pltpu
from jax.sharding import PartitionSpec as P

PAIRS = 5
FIELDS = 9
AXES = ("shot", "gx", "gy")
TRI = [(i, j) for i in range(PAIRS) for j in range(i, PAIRS)]
SLOTS = 2 * len(TRI) + 2 * PAIRS
GROUPS = -(-SLOTS // 8)


LIMIT = 4 << 20

VMEM = pl.BlockSpec(memory_space=pltpu.VMEM)


def call(kernel, out_shapes, args, scratch=()):
    out = [jax.ShapeDtypeStruct(shape, jnp.float32) for shape in out_shapes]
    return pl.pallas_call(
        kernel,
        out_shape=out,
        in_specs=[VMEM] * len(args),
        out_specs=[VMEM] * len(out),
        scratch_shapes=[pltpu.VMEM(shape, jnp.float32) for shape in scratch],
        compiler_params=pltpu.CompilerParams(vmem_limit_bytes=LIMIT),
    )(*args)


def power_of_two(n):
    return n & (n - 1) == 0


def lanes(shape):
    return lax.broadcasted_iota(jnp.int32, shape, len(shape) - 1)


def sum_kernel(scale, ends, count, *refs):
    blocks, fields_ref, cols = refs[:count], refs[count], refs[count + 1 :]
    levels, rows, width = fields_ref.shape[1:]
    lane = lanes((rows, width))
    for level in range(levels):
        packed = [jnp.zeros((rows, width), jnp.float32) for _ in cols]
        for f in range(FIELDS):
            total = blocks[0][f, level]
            for block in blocks[1:]:
                total = total + block[f, level]
            total = total * scale
            fields_ref[f, level] = total
            for k, end in enumerate(ends()):
                moved = pltpu.roll(total, (f + width - end) % width, 1)
                packed[k] = jnp.where(lane == f, moved, packed[k])
        for k, col in enumerate(cols):
            col[level] = packed[k]


def along_y_kernel(slots, fields_ref, *refs):
    received, (out_ref, first_ref, last_ref) = refs[:-3], refs[-3:]
    levels, rows, width = fields_ref.shape[1:]
    lane = lanes((rows, width))
    targets = slots()
    for level in range(levels):
        for f in range(FIELDS):
            own = fields_ref[f, level]
            left = jnp.where(lane == 0, 0.0, pltpu.roll(own, 1, 1))
            right = jnp.where(lane == width - 1, 0.0, pltpu.roll(own, width - 1, 1))
            for ref, (target, valid) in zip(received, targets):
                moved = pltpu.roll(ref[level], (target + width - f) % width, 1)
                hit = lane == target
                if valid is not None:
                    hit = jnp.logical_and(hit, valid)
                left = left + jnp.where(hit, moved, 0.0)
            value = 0.25 * (left + 2.0 * own + right)
            out_ref[f, level] = value
            first_ref[level, f : f + 1] = value[0:1]
            last_ref[level, f : f + 1] = value[rows - 1 : rows]


def dots_kernel(filtered_ref, above_ref, below_ref, s_ref, y_ref, solved_ref, part_ref, slot_ref):
    levels, rows, width = filtered_ref.shape[1:]
    sub = lax.broadcasted_iota(jnp.int32, (rows, width), 0)
    at = lax.axis_index("gx")
    has_above = jnp.where(at > 0, 1.0, 0.0)
    has_below = jnp.where(at < lax.axis_size("gx") - 1, 1.0, 0.0)
    sums = [None] * SLOTS

    def add(slot, value):
        sums[slot] = value if sums[slot] is None else sums[slot] + value

    for level in range(levels):
        smooth = []
        for f in range(FIELDS):
            own = filtered_ref[f, level]
            above = jnp.broadcast_to(above_ref[level, f : f + 1] * has_above, own.shape)
            below = jnp.broadcast_to(below_ref[level, f : f + 1] * has_below, own.shape)
            up = jnp.where(sub == 0, above, pltpu.roll(own, 1, 0))
            down = jnp.where(sub == rows - 1, below, pltpu.roll(own, rows - 1, 0))
            smooth.append(0.25 * (up + 2.0 * own + down))
        grad = smooth[0:3]
        diag_p, diag_s, diag_r, cross_ps, cross_pr, cross_sr = smooth[3:9]
        cof_pp = diag_s * diag_r - cross_sr * cross_sr
        cof_ps = cross_pr * cross_sr - cross_ps * diag_r
        cof_pr = cross_ps * cross_sr - diag_s * cross_pr
        cof_ss = diag_p * diag_r - cross_pr * cross_pr
        cof_sr = cross_ps * cross_pr - diag_p * cross_sr
        cof_rr = diag_p * diag_s - cross_ps * cross_ps
        determinant = diag_p * cof_pp + cross_ps * cof_ps + cross_pr * cof_pr
        inverse_det = 1.0 / determinant

        def solve(vec):
            one, two, three = vec
            return [
                (cof_pp * one + cof_ps * two + cof_pr * three) * inverse_det,
                (cof_ps * one + cof_ss * two + cof_sr * three) * inverse_det,
                (cof_pr * one + cof_sr * two + cof_rr * three) * inverse_det,
            ]

        def dot(a, b):
            return a[0] * b[0] + a[1] * b[1] + a[2] * b[2]

        s = [[s_ref[i, p, level] for p in range(3)] for i in range(PAIRS)]
        y = [[y_ref[i, p, level] for p in range(3)] for i in range(PAIRS)]
        newton = solve(grad)
        for p in range(3):
            solved_ref[0, p, level] = newton[p]
        for j in range(PAIRS):
            z = solve(y[j])
            for p in range(3):
                solved_ref[1 + j, p, level] = z[p]
            for i in range(j + 1):
                add(TRI.index((i, j)), dot(s[i], y[j]))
                add(len(TRI) + TRI.index((i, j)), dot(y[i], z))
            add(2 * len(TRI) + j, dot(s[j], grad))
            add(2 * len(TRI) + PAIRS + j, dot(y[j], newton))

    for slot in range(8 * GROUPS):
        value = sums[slot] if slot < SLOTS else jnp.zeros((rows, width), jnp.float32)
        slot_ref[slot * rows : (slot + 1) * rows] = value
    lane = lanes((8, width))
    packed = jnp.zeros((8, width), jnp.float32)
    for group in range(GROUPS):
        total = None
        for r in range(rows):
            piece = slot_ref[pl.ds(group * 8 * rows + r, 8, stride=rows)]
            total = piece if total is None else total + piece
        packed = jnp.where(lane == group, jnp.sum(total, axis=1, keepdims=True), packed)
    part_ref[...] = packed


def combine_kernel(count, *refs):
    parts, (solved_ref, s_ref, out_ref, spread_ref) = refs[:count], refs[count:]
    levels, rows, width = s_ref.shape[2:]
    packed = parts[0][...]
    for part in parts[1:]:
        packed = packed + part[...]
    for group in range(GROUPS):
        spread_ref[group * 8 : (group + 1) * 8] = jnp.broadcast_to(
            packed[:, group : group + 1], (8, width)
        )

    def entry(slot):
        return spread_ref[slot : slot + 1]

    cross = {pair: entry(k) for k, pair in enumerate(TRI)}
    curv = {pair: entry(len(TRI) + k) for k, pair in enumerate(TRI)}
    hist_dot = [entry(2 * len(TRI) + i) for i in range(PAIRS)]
    pre_dot = [entry(2 * len(TRI) + PAIRS + i) for i in range(PAIRS)]
    inverse = [1.0 / cross[i, i] for i in range(PAIRS)]
    coef_p = [None] * PAIRS
    for row in range(PAIRS - 1, -1, -1):
        total = hist_dot[row]
        for col in range(PAIRS - 1, row, -1):
            total = total - cross[row, col] * coef_p[col]
        coef_p[row] = total * inverse[row]
    coef_q = [None] * PAIRS
    for row in range(PAIRS):
        total = cross[row, row] * coef_p[row] - pre_dot[row]
        for col in range(PAIRS):
            total = total + curv[min(row, col), max(row, col)] * coef_p[col]
        for col in range(row):
            total = total - cross[col, row] * coef_q[col]
        coef_q[row] = total * inverse[row]
    coef_p = [jnp.broadcast_to(c, (rows, width)) for c in coef_p]
    coef_q = [jnp.broadcast_to(c, (rows, width)) for c in coef_q]
    for p in range(3):
        for level in range(levels):
            total = solved_ref[0, p, level]
            for i in range(PAIRS):
                total = total + coef_q[i] * s_ref[i, p, level]
                total = total - coef_p[i] * solved_ref[1 + i, p, level]
            out_ref[p, level] = -total


def shifted(x, axis, step):
    n = lax.axis_size(axis)
    return lax.ppermute(x, axis, [(i, (i + step) % n) for i in range(n)])


def flipped(x, flips):
    sizes = [lax.axis_size(a) for a in AXES]
    pairs = []
    for i in range(sizes[0]):
        for j in range(sizes[1]):
            for k in range(sizes[2]):
                to = [a ^ flips.get(n, 0) for n, a in zip(AXES, (i, j, k))]
                pairs.append(
                    (
                        (i * sizes[1] + j) * sizes[2] + k,
                        (to[0] * sizes[1] + to[1]) * sizes[2] + to[2],
                    )
                )
    return lax.ppermute(x, AXES, pairs)


def shot_blocks(partials):
    n = lax.axis_size("shot")
    levels = partials.shape[1] // n
    if n > 8 or not power_of_two(n):
        return [lax.psum_scatter(partials, "shot", scatter_dimension=1, tiled=True)]
    me = lax.axis_index("shot")

    def block(k):
        return lax.dynamic_slice_in_dim(partials, (me ^ k) * levels, levels, axis=1)

    blocks = [block(0)]
    for k in range(n - 1, 0, -1):
        blocks.append(flipped(block(k), {"shot": k}))
    return blocks


def all_sums(part):
    if not all(power_of_two(lax.axis_size(a)) for a in AXES):
        return [lax.psum(part, AXES)]
    bits = {a: [1 << b for b in range(lax.axis_size(a).bit_length() - 1)] for a in AXES}
    stages = []
    for bit in bits["shot"][:0:-1]:
        stages.append([{"shot": bit}])
    last = bits["shot"][:1]
    flips = [{"gy": m} for m in bits["gy"][:1]] + [{"shot": m} for m in last]
    if len(flips) == 2:
        flips.append({**flips[0], **flips[1]})
    stages.append(flips)
    for bit in bits["gy"][1:]:
        stages.append([{"gy": bit}])
    stages.append([{"gx": m} for m in range(1, lax.axis_size("gx"))])
    pieces = [part]
    for stage in stages:
        if not stage:
            continue
        part = functools.reduce(jnp.add, pieces)
        pieces = [part] + [flipped(part, flip) for flip in stage]
    return pieces


def per_device(partials, hist_s, hist_y):
    levels, rows, width = hist_s.shape[2:]
    blocks = shot_blocks(partials[0])
    scale = 1.0 / lax.axis_size("shot")
    n_y = lax.axis_size("gy")
    tile = (FIELDS, levels, rows, width)
    col = (levels, rows, width)

    if n_y == 2:
        def ends():
            return [jnp.where(lax.axis_index("gy") == 0, width - 1, 0)]

        def slots():
            return [(jnp.where(lax.axis_index("gy") == 0, width - 1, 0), None)]
    else:

        def ends():
            return [0, width - 1]

        def slots():
            at = lax.axis_index("gy")
            return [(width - 1, at < n_y - 1), (0, at > 0)]

    sends = 1 if n_y == 2 else 2
    fields, *cols = call(
        functools.partial(sum_kernel, scale, ends, len(blocks)), [tile] + [col] * sends, blocks
    )
    if n_y == 2:
        received = [shifted(cols[0], "gy", 1)]
    else:
        received = [shifted(cols[0], "gy", -1), shifted(cols[1], "gy", 1)]
    edge = (levels, FIELDS, width)
    filtered, first, last = call(
        functools.partial(along_y_kernel, slots), [tile, edge, edge], [fields] + received
    )
    above = shifted(last, "gx", 1)
    below = shifted(first, "gx", -1)
    solved, part = call(
        dots_kernel,
        [(1 + PAIRS, 3, levels, rows, width), (8, width)],
        [filtered, above, below, hist_s, hist_y],
        [(8 * GROUPS * rows, width)],
    )
    pieces = all_sums(part)
    (direction,) = call(
        functools.partial(combine_kernel, len(pieces)),
        [(3, levels, rows, width)],
        pieces + [solved, hist_s],
        [(8 * GROUPS, width)],
    )
    return direction


def solution(mesh):
    return jax.shard_map(
        per_device,
        mesh=mesh,
        in_specs=(
            P("shot", None, None, "gx", "gy"),
            P(None, None, "shot", "gx", "gy"),
            P(None, None, "shot", "gx", "gy"),
        ),
        out_specs=P(None, "shot", "gx", "gy"),
        check_vma=False,
    )
```

```python
import functools

import jax
import jax.numpy as jnp
from jax import lax
from jax.experimental import pallas as pl
from jax.experimental.pallas import tpu as pltpu
from jax.sharding import PartitionSpec as P

PAIRS = 5
FIELDS = 9
AXES = ("shot", "gx", "gy")
TRI = [(i, j) for i in range(PAIRS) for j in range(i, PAIRS)]
N_TRI = len(TRI)
FIRST = -(-N_TRI // 8)
LATER = -(-(N_TRI + 2 * PAIRS) // 8)
GROUPS = FIRST + LATER
BESIDE = FIELDS
HISTORY = 2 * FIELDS
HALF = 64
LIMIT = 4 << 20
SORDER = (2, 3, 1)
STAGES = [[{'gx': 1}], [{'gx': 3}], [{'shot': 3, 'gx': 1}, {'shot': 2, 'gx': 1}, {'shot': 1, 'gx': 1}]]


VMEM = pl.BlockSpec(memory_space=pltpu.VMEM)


def call(kernel, out_shapes, args, scratch=()):
    out = [jax.ShapeDtypeStruct(shape, jnp.float32) for shape in out_shapes]
    return pl.pallas_call(
        kernel,
        out_shape=out,
        in_specs=[VMEM] * len(args),
        out_specs=[VMEM] * len(out),
        scratch_shapes=[pltpu.VMEM(shape, jnp.float32) for shape in scratch],
        compiler_params=pltpu.CompilerParams(vmem_limit_bytes=LIMIT),
    )(*args)


def iota(shape, dim):
    return lax.broadcasted_iota(jnp.int32, shape, dim)


def edge_lane(width):
    first = lax.axis_index("gy") == 0
    return jnp.where(first, width - 1, 0), jnp.where(first, -1, 1)


def dot(a, b):
    return a[0] * b[0] + a[1] * b[1] + a[2] * b[2]


def inverse(hessian):
    diag_p, diag_s, diag_r, cross_ps, cross_pr, cross_sr = hessian
    cof_pp = diag_s * diag_r - cross_sr * cross_sr
    cof_ps = cross_pr * cross_sr - cross_ps * diag_r
    cof_pr = cross_ps * cross_sr - diag_s * cross_pr
    cof_ss = diag_p * diag_r - cross_pr * cross_pr
    cof_sr = cross_ps * cross_pr - diag_p * cross_sr
    cof_rr = diag_p * diag_s - cross_ps * cross_ps
    determinant = diag_p * cof_pp + cross_ps * cof_ps + cross_pr * cof_pr
    inverse_det = 1.0 / determinant
    return [c * inverse_det for c in (cof_pp, cof_ps, cof_pr, cof_ss, cof_sr, cof_rr)]


def applied(inv, vec):
    one, two, three = vec
    return [
        inv[0] * one + inv[1] * two + inv[2] * three,
        inv[1] * one + inv[3] * two + inv[4] * three,
        inv[2] * one + inv[4] * two + inv[5] * three,
    ]


def later_sums(smooth, s, y):
    grad = smooth[0:3]
    inv = inverse(smooth[3:9])
    newton = applied(inv, grad)
    terms = [None] * (N_TRI + 2 * PAIRS)
    for j in range(PAIRS):
        z = applied(inv, y[j])
        for i in range(j + 1):
            terms[TRI.index((i, j))] = dot(y[i], z)
        terms[N_TRI + j] = dot(s[j], grad)
        terms[N_TRI + PAIRS + j] = dot(y[j], newton)
    return terms


def added(sums, terms):
    return terms if sums is None else [a + b for a, b in zip(sums, terms)]


def packed_sums(sums, slots, group):
    rows, width = sums[0].shape
    groups = -(-len(sums) // 8)
    for k in range(8 * groups):
        slots[k * rows : (k + 1) * rows] = sums[k] if k < len(sums) else jnp.zeros((rows, width))
    lane = iota((8, width), 1)
    packed = jnp.zeros((8, width), jnp.float32)
    for g in range(groups):
        total = slots[pl.ds(g * 8 * rows, 8, stride=rows)]
        for r in range(1, rows):
            total = total + slots[pl.ds(g * 8 * rows + r, 8, stride=rows)]
        packed = jnp.where(lane == group + g, jnp.sum(total, axis=1, keepdims=True), packed)
    return packed


def history_kernel(s_ref, y_ref, column_ref, part_ref, slots):
    levels, rows, width = s_ref.shape[2:]
    edge, _ = edge_lane(width)
    lane = iota((rows, width), 1)
    sums = None
    for level in range(levels):
        s = [[s_ref[i, p, level] for p in range(3)] for i in range(PAIRS)]
        y = [[y_ref[i, p, level] for p in range(3)] for i in range(PAIRS)]
        column = jnp.zeros((rows, width), jnp.float32)
        for k, value in enumerate(sum(s, []) + sum(y, [])):
            at = HISTORY + k
            column = jnp.where(lane == at, pltpu.roll(value, (at + width - edge) % width, 1), column)
        column_ref[level] = column
        sums = added(sums, [dot(s[i], y[j]) for i, j in TRI])
    part_ref[...] = packed_sums(sums, slots, 0)


def sum_kernel(scale, count, *refs):
    blocks, (fields_ref, first_ref, last_ref) = refs[:count], refs[count:]
    levels, rows = fields_ref.shape[1:3]
    for level in range(levels):
        for f in range(FIELDS):
            total = blocks[0][f, level]
            for block in blocks[1:]:
                total = total + block[f, level]
            total = total * scale
            fields_ref[f, level] = total
            first_ref[level, f : f + 1] = total[0:1]
            last_ref[level, f : f + 1] = total[rows - 1 : rows]


def along_y(own, halo=None):
    width = own.shape[-1]
    lane = iota(own.shape, 1)
    left = jnp.where(lane == 0, 0.0, pltpu.roll(own, 1, 1))
    right = jnp.where(lane == width - 1, 0.0, pltpu.roll(own, width - 1, 1))
    if halo is not None:
        left = left + halo
    return 0.25 * (left + 2.0 * own + right)


def main_kernel(
    fields_ref, above_ref, below_ref, s_ref, y_ref, column_ref, cross_ref, along_ref, send_ref, slots
):
    levels, rows, width = fields_ref.shape[1:]
    edge, step = edge_lane(width)
    sub = iota((rows, width), 0)
    lane = iota((rows, width), 1)
    at = lax.axis_index("gx")
    has_above = at > 0
    has_below = at < lax.axis_size("gx") - 1
    sums = None
    for level in range(levels):
        column = column_ref[level]
        smooth = []
        for f in range(FIELDS):
            own = fields_ref[f, level]
            above = jnp.where(has_above, above_ref[level, f : f + 1], 0.0)
            below = jnp.where(has_below, below_ref[level, f : f + 1], 0.0)
            up = jnp.where(sub == 0, jnp.broadcast_to(above, own.shape), pltpu.roll(own, 1, 0))
            down = jnp.where(
                sub == rows - 1, jnp.broadcast_to(below, own.shape), pltpu.roll(own, rows - 1, 0)
            )
            value = 0.25 * (up + 2.0 * own + down)
            along_ref[f, level] = value
            moved = pltpu.roll(value, (f + width - edge) % width, 1)
            column = jnp.where(lane == f, moved, column)
            moved = pltpu.roll(value, (BESIDE + f + width - edge - step) % width, 1)
            column = jnp.where(lane == BESIDE + f, moved, column)
            smooth.append(along_y(value))
        send_ref[level] = column
        s = [[s_ref[i, p, level] for p in range(3)] for i in range(PAIRS)]
        y = [[y_ref[i, p, level] for p in range(3)] for i in range(PAIRS)]
        sums = added(sums, later_sums(smooth, s, y))
    inside = lane != edge
    sums = [jnp.where(inside, total, 0.0) for total in sums]
    send_ref[levels] = cross_ref[...] + packed_sums(sums, slots, FIRST)


def edge_kernel(own_ref, other_ref, part_ref, slots):
    levels, rows, width = own_ref.shape
    levels -= 1
    lane = iota((rows, width), 1)
    sums = None
    for level in range(levels):
        own, other = own_ref[level], other_ref[level]
        own_edge = 0.25 * (pltpu.roll(own, width - BESIDE, 1) + 2.0 * own + other)
        other_edge = 0.25 * (pltpu.roll(other, width - BESIDE, 1) + 2.0 * other + own)
        fields = jnp.where(lane < HALF, own_edge, pltpu.roll(other_edge, HALF, 1))
        history = jnp.where(lane < HALF, own, pltpu.roll(other, HALF, 1))

        def entry(array, k):
            return array if k == 0 else pltpu.roll(array, width - k, 1)

        smooth = [entry(fields, f) for f in range(FIELDS)]
        vectors = [entry(history, HISTORY + k) for k in range(6 * PAIRS)]
        vectors = [vectors[k : k + 3] for k in range(0, 6 * PAIRS, 3)]
        sums = added(sums, later_sums(smooth, vectors[:PAIRS], vectors[PAIRS:]))
    cells = jnp.logical_or(lane == 0, lane == HALF)
    sums = [jnp.where(cells, total, 0.0) for total in sums]
    part_ref[...] = own_ref[levels] + other_ref[levels] + packed_sums(sums, slots, FIRST)


def cells_kernel(along_ref, other_ref, cells_ref):
    levels, rows, width = along_ref.shape[1:]
    edge, _ = edge_lane(width)
    lane = iota((rows, width), 1)
    for level in range(levels):
        smooth = []
        for f in range(FIELDS):
            moved = pltpu.roll(other_ref[level], (edge + width - f) % width, 1)
            smooth.append(along_y(along_ref[f, level], jnp.where(lane == edge, moved, 0.0)))
        for k, value in enumerate(smooth[0:3] + inverse(smooth[3:9])):
            cells_ref[k, level] = value


def combine_kernel(count, *refs):
    parts, (cells_ref, s_ref, y_ref, out_ref, spread_ref) = refs[:count], refs[count:]
    levels, rows, width = s_ref.shape[2:]
    packed = parts[0][...]
    for part in parts[1:]:
        packed = packed + part[...]
    for g in range(GROUPS):
        spread_ref[g * 8 : (g + 1) * 8] = jnp.broadcast_to(packed[:, g : g + 1], (8, width))

    def entry(k, group=0):
        return spread_ref[8 * group + k : 8 * group + k + 1]

    cross = {pair: entry(k) for k, pair in enumerate(TRI)}
    curv = {pair: entry(k, FIRST) for k, pair in enumerate(TRI)}
    hist_dot = [entry(N_TRI + i, FIRST) for i in range(PAIRS)]
    pre_dot = [entry(N_TRI + PAIRS + i, FIRST) for i in range(PAIRS)]
    scale = [1.0 / cross[i, i] for i in range(PAIRS)]
    coef_p = [None] * PAIRS
    for row in range(PAIRS - 1, -1, -1):
        total = hist_dot[row]
        for col in range(PAIRS - 1, row, -1):
            total = total - cross[row, col] * coef_p[col]
        coef_p[row] = total * scale[row]
    coef_q = [None] * PAIRS
    for row in range(PAIRS):
        total = cross[row, row] * coef_p[row] - pre_dot[row]
        for col in range(PAIRS):
            total = total + curv[min(row, col), max(row, col)] * coef_p[col]
        for col in range(row):
            total = total - cross[col, row] * coef_q[col]
        coef_q[row] = total * scale[row]
    coef_p = [jnp.broadcast_to(c, (rows, width)) for c in coef_p]
    coef_q = [jnp.broadcast_to(c, (rows, width)) for c in coef_q]
    for level in range(levels):
        rest = []
        for p in range(3):
            total = cells_ref[p, level]
            for i in range(PAIRS):
                total = total - coef_p[i] * y_ref[i, p, level]
            rest.append(total)
        solved = applied([cells_ref[3 + k, level] for k in range(6)], rest)
        for p in range(3):
            total = solved[p]
            for i in range(PAIRS):
                total = total + coef_q[i] * s_ref[i, p, level]
            out_ref[p, level] = -total


def flipped(x, flips):
    sizes = [lax.axis_size(a) for a in AXES]
    pairs = []
    for i in range(sizes[0]):
        for j in range(sizes[1]):
            for k in range(sizes[2]):
                to = [a ^ flips.get(n, 0) for n, a in zip(AXES, (i, j, k))]
                pairs.append(
                    (
                        (i * sizes[1] + j) * sizes[2] + k,
                        (to[0] * sizes[1] + to[1]) * sizes[2] + to[2],
                    )
                )
    return lax.ppermute(x, AXES, pairs)


def shot_blocks(partials):
    n = lax.axis_size("shot")
    levels = partials.shape[1] // n
    me = lax.axis_index("shot")

    def block(k):
        return lax.dynamic_slice_in_dim(partials, (me ^ k) * levels, levels, axis=1)

    mine = [block(k) for k in range(n)]
    blocks = [mine[0]]
    for k in SORDER:
        blocks.append(flipped(mine[k], {"shot": k}))
    return blocks


def all_sums(part):
    pieces = [part]
    for stage in STAGES:
        part = functools.reduce(jnp.add, pieces)
        pieces = [part]
        for flip in stage:
            pieces.append(flipped(part, flip))
    return pieces


def exchanged(partials, hist_s, hist_y):
    levels, rows, width = hist_s.shape[2:]
    scale = 1.0 / lax.axis_size("shot")
    n_x = lax.axis_size("gx")
    tile = (FIELDS, levels, rows, width)
    edge = (levels, FIELDS, width)
    blocks = shot_blocks(partials[0])
    column, cross = call(
        history_kernel,
        [(levels, rows, width), (8, width)],
        [hist_s, hist_y],
        [(8 * FIRST * rows, width)],
    )
    fields, first, last = call(
        functools.partial(sum_kernel, scale, len(blocks)), [tile, edge, edge], blocks
    )
    above = lax.ppermute(last, "gx", [(i, (i + 1) % n_x) for i in range(n_x)])
    below = lax.ppermute(first, "gx", [((i + 1) % n_x, i) for i in range(n_x)])
    along, send = call(
        main_kernel,
        [tile, (levels + 1, rows, width)],
        [fields, above, below, hist_s, hist_y, column, cross],
        [(8 * LATER * rows, width)],
    )
    other = flipped(send, {"gy": 1})
    (part,) = call(edge_kernel, [(rows, width)], [send, other], [(8 * LATER * rows, width)])
    (cells,) = call(cells_kernel, [tile], [along, other])
    pieces = all_sums(part)
    (direction,) = call(
        functools.partial(combine_kernel, len(pieces)),
        [(3, levels, rows, width)],
        pieces + [cells, hist_s, hist_y],
        [(8 * GROUPS, width)],
    )
    return direction


def extended_2(cells, sides, width):
    for axis, dim in sides:
        count = lax.axis_size(axis)
        ends = count - 1
        head = lax.slice_in_dim(cells, 0, width, axis=dim)
        tail = lax.slice_in_dim(cells, cells.shape[dim] - width, cells.shape[dim], axis=dim)
        cells = jnp.concatenate(
            [
                lax.ppermute(tail, axis, [(i, (i + 1) % count) for i in range(ends)]),
                cells,
                lax.ppermute(head, axis, [((i + 1) % count, i) for i in range(ends)]),
            ],
            axis=dim,
        )
    return cells


def smooth_block(padded):
    along_x = 0.25 * (padded[:, :, :-2] + 2.0 * padded[:, :, 1:-1] + padded[:, :, 2:])
    return 0.25 * (along_x[..., :-2] + 2.0 * along_x[..., 1:-1] + along_x[..., 2:])


def apply_inverse(hessian, vectors):
    diag_p = hessian[0]
    diag_s = hessian[1]
    diag_r = hessian[2]
    cross_ps = hessian[3]
    cross_pr = hessian[4]
    cross_sr = hessian[5]
    cof_pp = diag_s * diag_r - cross_sr * cross_sr
    cof_ps = cross_pr * cross_sr - cross_ps * diag_r
    cof_pr = cross_ps * cross_sr - diag_s * cross_pr
    cof_ss = diag_p * diag_r - cross_pr * cross_pr
    cof_sr = cross_ps * cross_pr - diag_p * cross_sr
    cof_rr = diag_p * diag_s - cross_ps * cross_ps
    determinant = diag_p * cof_pp + cross_ps * cof_ps + cross_pr * cof_pr
    inverse_det = 1.0 / determinant
    comp_one = vectors[:, 0]
    comp_two = vectors[:, 1]
    comp_three = vectors[:, 2]
    return jnp.stack(
        [
            (cof_pp * comp_one + cof_ps * comp_two + cof_pr * comp_three) * inverse_det,
            (cof_ps * comp_one + cof_ss * comp_two + cof_sr * comp_three) * inverse_det,
            (cof_pr * comp_one + cof_sr * comp_two + cof_rr * comp_three) * inverse_det,
        ],
        axis=1,
    )


def pair_dots(left_flat, right_flat):
    return lax.dot_general(
        left_flat,
        right_flat,
        (((1,), (1,)), ((), ())),
        precision=lax.Precision.HIGHEST,
        preferred_element_type=jnp.float32,
    )


def upper_solve(matrix, values):
    count = matrix.shape[0]
    found = [None] * count
    for row in range(count - 1, -1, -1):
        total = values[row]
        for col in range(row + 1, count):
            total = total - matrix[row, col] * found[col]
        found[row] = total / matrix[row, row]
    return jnp.stack(found)


def upper_transpose_solve(matrix, values):
    count = matrix.shape[0]
    found = [None] * count
    for row in range(count):
        total = values[row]
        for col in range(row):
            total = total - matrix[col, row] * found[col]
        found[row] = total / matrix[row, row]
    return jnp.stack(found)


def combine_terms(cross_gram, curv_gram, hist_dot, pre_dot, solved, hist_s):
    middle_part = jnp.diag(jnp.diag(cross_gram)) + curv_gram
    coef_p = upper_solve(cross_gram, hist_dot)
    right_hand = jnp.dot(middle_part, coef_p, precision=lax.Precision.HIGHEST) - pre_dot
    coef_q = upper_transpose_solve(cross_gram, right_hand)
    update_s = jnp.tensordot(coef_q, hist_s, axes=1, precision=lax.Precision.HIGHEST)
    update_z = jnp.tensordot(coef_p, solved[1:], axes=1, precision=lax.Precision.HIGHEST)
    return -(solved[0] + update_s - update_z)


def plain_device(partials, hist_s, hist_y):
    s_flat = hist_s.reshape(PAIRS, -1)
    y_flat = hist_y.reshape(PAIRS, -1)
    inverse_count = 1.0 / lax.axis_size("shot")
    level_sums = lax.psum_scatter(partials[0], "shot", scatter_dimension=1, tiled=True)
    fields = level_sums * inverse_count
    extended = extended_2(fields, (("gx", 2), ("gy", 3)), 1)
    smoothed = smooth_block(extended)
    gradient = smoothed[0:3]
    solved = apply_inverse(smoothed[3:9], jnp.concatenate([gradient[None], hist_y], axis=0))
    z_flat = solved[1:].reshape(PAIRS, -1)
    curv_part = pair_dots(y_flat, z_flat)
    hist_part = pair_dots(s_flat, gradient.reshape(1, -1))[:, 0]
    pre_part = pair_dots(y_flat, solved[0].reshape(1, -1))[:, 0]
    cross_gram, curv_gram, hist_dot, pre_dot = lax.psum(
        (pair_dots(s_flat, y_flat), curv_part, hist_part, pre_part), ("shot", "gx", "gy")
    )
    return combine_terms(cross_gram, curv_gram, hist_dot, pre_dot, solved, hist_s)


def per_device(*args):
    return exchanged(*args)


def solution(mesh):
    sizes = [mesh.shape[a] for a in AXES]
    fits = sizes[0] == 4 and sizes[1] == 4 and sizes[2] == 2
    return jax.shard_map(
        per_device if fits else plain_device,
        mesh=mesh,
        in_specs=(
            P("shot", None, None, "gx", "gy"),
            P(None, None, "shot", "gx", "gy"),
            P(None, None, "shot", "gx", "gy"),
        ),
        out_specs=P(None, "shot", "gx", "gy"),
        check_vma=False,
    )
```

```python
import functools

import jax
import jax.numpy as jnp
from jax import lax
from jax.experimental import pallas as pl
from jax.experimental.pallas import tpu as pltpu
from jax.sharding import PartitionSpec as P

PAIRS = 5
FIELDS = 9
AXES = ("shot", "gx", "gy")
TRI = [(i, j) for i in range(PAIRS) for j in range(i, PAIRS)]
N_TRI = len(TRI)
FIRST = -(-N_TRI // 8)
LATER = -(-(N_TRI + 2 * PAIRS) // 8)
GROUPS = FIRST + LATER
BESIDE = FIELDS
SUMS = 2 * FIELDS
BLOCK = 32
LIMIT = 4 << 20


VMEM = pl.BlockSpec(memory_space=pltpu.VMEM)


def call(kernel, out_shapes, args, scratch=()):
    out = [jax.ShapeDtypeStruct(shape, jnp.float32) for shape in out_shapes]
    return pl.pallas_call(
        kernel,
        out_shape=out,
        in_specs=[VMEM] * len(args),
        out_specs=[VMEM] * len(out),
        scratch_shapes=[pltpu.VMEM(shape, jnp.float32) for shape in scratch],
        compiler_params=pltpu.CompilerParams(vmem_limit_bytes=LIMIT),
    )(*args)


def iota(shape, dim):
    return lax.broadcasted_iota(jnp.int32, shape, dim)


def edge_lane(width):
    first = lax.axis_index("gy") == 0
    return jnp.where(first, width - 1, 0), jnp.where(first, -1, 1)


def block_lane():
    return BLOCK * (2 * lax.axis_index("gy") + lax.axis_index("gx") % 2)


def dot(a, b):
    return a[0] * b[0] + a[1] * b[1] + a[2] * b[2]


def inverse(hessian):
    diag_p, diag_s, diag_r, cross_ps, cross_pr, cross_sr = hessian
    cof_pp = diag_s * diag_r - cross_sr * cross_sr
    cof_ps = cross_pr * cross_sr - cross_ps * diag_r
    cof_pr = cross_ps * cross_sr - diag_s * cross_pr
    cof_ss = diag_p * diag_r - cross_pr * cross_pr
    cof_sr = cross_ps * cross_pr - diag_p * cross_sr
    cof_rr = diag_p * diag_s - cross_ps * cross_ps
    determinant = diag_p * cof_pp + cross_ps * cof_ps + cross_pr * cof_pr
    inverse_det = 1.0 / determinant
    return [c * inverse_det for c in (cof_pp, cof_ps, cof_pr, cof_ss, cof_sr, cof_rr)]


def applied(inv, vec):
    one, two, three = vec
    return [
        inv[0] * one + inv[1] * two + inv[2] * three,
        inv[1] * one + inv[3] * two + inv[4] * three,
        inv[2] * one + inv[4] * two + inv[5] * three,
    ]


def later_sums(smooth, s, y):
    grad = smooth[0:3]
    inv = inverse(smooth[3:9])
    newton = applied(inv, grad)
    terms = [None] * (N_TRI + 2 * PAIRS)
    for j in range(PAIRS):
        z = applied(inv, y[j])
        for i in range(j + 1):
            terms[TRI.index((i, j))] = dot(y[i], z)
        terms[N_TRI + j] = dot(s[j], grad)
        terms[N_TRI + PAIRS + j] = dot(y[j], newton)
    return terms


def added(sums, terms):
    return terms if sums is None else [a + b for a, b in zip(sums, terms)]


def packed_sums(sums, slots, group):
    rows, width = sums[0].shape
    groups = -(-len(sums) // 8)
    for k in range(8 * groups):
        slots[k * rows : (k + 1) * rows] = sums[k] if k < len(sums) else jnp.zeros((rows, width))
    lane = iota((8, width), 1)
    packed = jnp.zeros((8, width), jnp.float32)
    group = group + SUMS
    for g in range(groups):
        total = slots[pl.ds(g * 8 * rows, 8, stride=rows)]
        for r in range(1, rows):
            total = total + slots[pl.ds(g * 8 * rows + r, 8, stride=rows)]
        packed = jnp.where(lane == group + g, jnp.sum(total, axis=1, keepdims=True), packed)
    return packed


def history_kernel(s_ref, y_ref, column_ref, part_ref, slots):
    levels, rows, width = s_ref.shape[2:]
    edge, _ = edge_lane(width)
    base = block_lane()
    lane = iota((rows, width), 1)
    sums = None
    for level in range(levels):
        s = [[s_ref[i, p, level] for p in range(3)] for i in range(PAIRS)]
        y = [[y_ref[i, p, level] for p in range(3)] for i in range(PAIRS)]
        column = jnp.zeros((rows, width), jnp.float32)
        for k, value in enumerate(sum(s, []) + sum(y, [])):
            at = base + k
            column = jnp.where(lane == at, pltpu.roll(value, (at + width - edge) % width, 1), column)
        column_ref[level] = column
        sums = added(sums, [dot(s[i], y[j]) for i, j in TRI])
    part_ref[...] = packed_sums(sums, slots, 0)


def sum_kernel(scale, count, *refs):
    blocks, (fields_ref, first_ref, last_ref) = refs[:count], refs[count:]
    levels, rows = fields_ref.shape[1:3]
    for level in range(levels):
        for f in range(FIELDS):
            total = blocks[0][f, level]
            for block in blocks[1:]:
                total = total + block[f, level]
            total = total * scale
            fields_ref[f, level] = total
            first_ref[level, f : f + 1] = total[0:1]
            last_ref[level, f : f + 1] = total[rows - 1 : rows]


def along_y(own, halo=None):
    width = own.shape[-1]
    lane = iota(own.shape, 1)
    left = jnp.where(lane == 0, 0.0, pltpu.roll(own, 1, 1))
    right = jnp.where(lane == width - 1, 0.0, pltpu.roll(own, width - 1, 1))
    if halo is not None:
        left = left + halo
    return 0.25 * (left + 2.0 * own + right)


def main_kernel(
    fields_ref, above_ref, below_ref, s_ref, y_ref, column_ref, cross_ref, along_ref, send_ref, slots
):
    levels, rows, width = fields_ref.shape[1:]
    edge, step = edge_lane(width)
    base = block_lane()
    sub = iota((rows, width), 0)
    lane = iota((rows, width), 1)
    at = lax.axis_index("gx")
    has_above = at > 0
    has_below = at < lax.axis_size("gx") - 1
    sums = None
    for level in range(levels):
        column = jnp.zeros((rows, width), jnp.float32)
        smooth = []
        for f in range(FIELDS):
            own = fields_ref[f, level]
            above = jnp.where(has_above, above_ref[level, f : f + 1], 0.0)
            below = jnp.where(has_below, below_ref[level, f : f + 1], 0.0)
            up = jnp.where(sub == 0, jnp.broadcast_to(above, own.shape), pltpu.roll(own, 1, 0))
            down = jnp.where(
                sub == rows - 1, jnp.broadcast_to(below, own.shape), pltpu.roll(own, rows - 1, 0)
            )
            value = 0.25 * (up + 2.0 * own + down)
            along_ref[f, level] = value
            at = base + f
            moved = pltpu.roll(value, (at + width - edge) % width, 1)
            column = jnp.where(lane == at, moved, column)
            moved = pltpu.roll(value, (at + BESIDE + width - edge - step) % width, 1)
            column = jnp.where(lane == at + BESIDE, moved, column)
            smooth.append(along_y(value))
        send_ref[0, level] = column
        send_ref[1, level] = column_ref[level]
        s = [[s_ref[i, p, level] for p in range(3)] for i in range(PAIRS)]
        y = [[y_ref[i, p, level] for p in range(3)] for i in range(PAIRS)]
        sums = added(sums, later_sums(smooth, s, y))
    inside = lane != edge
    sums = [jnp.where(inside, total, 0.0) for total in sums]
    send_ref[0, 0, 0:8] = send_ref[0, 0, 0:8] + cross_ref[...] + packed_sums(sums, slots, FIRST)


def edge_kernel(own_ref, other_ref, part_ref, other_column_ref, slots):
    levels, rows, width = own_ref.shape[1:]
    lane = iota((rows, width), 1)
    sums = None
    for level in range(levels):
        fields, history = [own_ref[k, level] + other_ref[k, level] for k in range(2)]
        across = pltpu.roll(fields, 2 * BLOCK, 1)
        other_column_ref[level] = across
        smooth = 0.25 * (pltpu.roll(fields, width - BESIDE, 1) + 2.0 * fields + across)
        if level == 0:
            part_ref[...] = fields

        def entry(array, k):
            return array if k == 0 else pltpu.roll(array, width - k, 1)

        smooth = [entry(smooth, f) for f in range(FIELDS)]
        vectors = [entry(history, k) for k in range(6 * PAIRS)]
        vectors = [vectors[k : k + 3] for k in range(0, 6 * PAIRS, 3)]
        sums = added(sums, later_sums(smooth, vectors[:PAIRS], vectors[PAIRS:]))
    cells = lane % BLOCK == 0
    sums = [jnp.where(cells, total, 0.0) for total in sums]
    part_ref[0:8] = part_ref[0:8] + packed_sums(sums, slots, FIRST)


def cells_kernel(along_ref, other_ref, cells_ref):
    levels, rows, width = along_ref.shape[1:]
    edge, _ = edge_lane(width)
    base = block_lane()
    lane = iota((rows, width), 1)
    for level in range(levels):
        smooth = []
        for f in range(FIELDS):
            moved = pltpu.roll(other_ref[level], (edge + 2 * width - base - f) % width, 1)
            smooth.append(along_y(along_ref[f, level], jnp.where(lane == edge, moved, 0.0)))
        for k, value in enumerate(smooth[0:3] + inverse(smooth[3:9])):
            cells_ref[k, level] = value


def combine_kernel(count, *refs):
    parts, (cells_ref, s_ref, y_ref, out_ref, spread_ref) = refs[:count], refs[count:]
    levels, rows, width = s_ref.shape[2:]
    packed = parts[0][...]
    for part in parts[1:]:
        packed = packed + part[...]
    for g in range(GROUPS):
        spread_ref[g * 8 : (g + 1) * 8] = jnp.broadcast_to(packed[0:8, SUMS + g : SUMS + g + 1], (8, width))

    def entry(k, group=0):
        return spread_ref[8 * group + k : 8 * group + k + 1]

    cross = {pair: entry(k) for k, pair in enumerate(TRI)}
    curv = {pair: entry(k, FIRST) for k, pair in enumerate(TRI)}
    hist_dot = [entry(N_TRI + i, FIRST) for i in range(PAIRS)]
    pre_dot = [entry(N_TRI + PAIRS + i, FIRST) for i in range(PAIRS)]
    scale = [1.0 / cross[i, i] for i in range(PAIRS)]
    coef_p = [None] * PAIRS
    for row in range(PAIRS - 1, -1, -1):
        total = hist_dot[row]
        for col in range(PAIRS - 1, row, -1):
            total = total - cross[row, col] * coef_p[col]
        coef_p[row] = total * scale[row]
    coef_q = [None] * PAIRS
    for row in range(PAIRS):
        total = cross[row, row] * coef_p[row] - pre_dot[row]
        for col in range(PAIRS):
            total = total + curv[min(row, col), max(row, col)] * coef_p[col]
        for col in range(row):
            total = total - cross[col, row] * coef_q[col]
        coef_q[row] = total * scale[row]
    coef_p = [jnp.broadcast_to(c, (rows, width)) for c in coef_p]
    coef_q = [jnp.broadcast_to(c, (rows, width)) for c in coef_q]
    for level in range(levels):
        rest = []
        for p in range(3):
            total = cells_ref[p, level]
            for i in range(PAIRS):
                total = total - coef_p[i] * y_ref[i, p, level]
            rest.append(total)
        solved = applied([cells_ref[3 + k, level] for k in range(6)], rest)
        for p in range(3):
            total = solved[p]
            for i in range(PAIRS):
                total = total + coef_q[i] * s_ref[i, p, level]
            out_ref[p, level] = -total


def flipped(x, flips):
    sizes = [lax.axis_size(a) for a in AXES]
    pairs = []
    for i in range(sizes[0]):
        for j in range(sizes[1]):
            for k in range(sizes[2]):
                to = [a ^ flips.get(n, 0) for n, a in zip(AXES, (i, j, k))]
                pairs.append(
                    (
                        (i * sizes[1] + j) * sizes[2] + k,
                        (to[0] * sizes[1] + to[1]) * sizes[2] + to[2],
                    )
                )
    return lax.ppermute(x, AXES, pairs)


def far_first(n):
    return range(n - 1, 0, -1)


def shot_blocks(partials):
    n = lax.axis_size("shot")
    levels = partials.shape[1] // n
    me = lax.axis_index("shot")

    def block(k):
        return lax.dynamic_slice_in_dim(partials, (me ^ k) * levels, levels, axis=1)

    mine = [block(k) for k in range(n)]
    blocks = [mine[0]]
    for k in far_first(n):
        blocks.append(flipped(mine[k], {"shot": k}))
    return blocks


def stages(sizes):
    n_shot, n_x = sizes
    return [[{"gx": m | 1} for m in range(2, n_x, 2)], [{"shot": k, "gx": 1} for k in far_first(n_shot)]]


def all_sums(part):
    pieces = [part]
    for stage in stages([lax.axis_size(a) for a in AXES[:2]]):
        part = functools.reduce(jnp.add, pieces)
        pieces = [part]
        for flip in stage:
            pieces.append(flipped(part, flip))
    return pieces


def exchanged(partials, hist_s, hist_y):
    levels, rows, width = hist_s.shape[2:]
    scale = 1.0 / lax.axis_size("shot")
    n_x = lax.axis_size("gx")
    tile = (FIELDS, levels, rows, width)
    edge = (levels, FIELDS, width)
    blocks = shot_blocks(partials[0])
    column, cross = call(
        history_kernel,
        [(levels, rows, width), (8, width)],
        [hist_s, hist_y],
        [(8 * FIRST * rows, width)],
    )
    fields, first, last = call(
        functools.partial(sum_kernel, scale, len(blocks)), [tile, edge, edge], blocks
    )
    below = lax.ppermute(first, "gx", [((i + 1) % n_x, i) for i in range(n_x)])
    above = lax.ppermute(last, "gx", [(i, (i + 1) % n_x) for i in range(n_x)])
    along, send = call(
        main_kernel,
        [tile, (2, levels, rows, width)],
        [fields, above, below, hist_s, hist_y, column, cross],
        [(8 * LATER * rows, width)],
    )
    send = send + flipped(send, {"gx": 1, "gy": 1})
    other = flipped(send, {"gx": 1})
    part, other_column = call(
        edge_kernel,
        [(rows, width), (levels, rows, width)],
        [send, other],
        [(8 * LATER * rows, width)],
    )
    (cells,) = call(cells_kernel, [tile], [along, other_column])
    pieces = all_sums(part)
    (direction,) = call(
        functools.partial(combine_kernel, len(pieces)),
        [(3, levels, rows, width)],
        pieces + [cells, hist_s, hist_y],
        [(8 * GROUPS, width)],
    )
    return direction


def extended_2(cells, sides, width):
    for axis, dim in sides:
        count = lax.axis_size(axis)
        ends = count - 1
        head = lax.slice_in_dim(cells, 0, width, axis=dim)
        tail = lax.slice_in_dim(cells, cells.shape[dim] - width, cells.shape[dim], axis=dim)
        cells = jnp.concatenate(
            [
                lax.ppermute(tail, axis, [(i, (i + 1) % count) for i in range(ends)]),
                cells,
                lax.ppermute(head, axis, [((i + 1) % count, i) for i in range(ends)]),
            ],
            axis=dim,
        )
    return cells


def smooth_block(padded):
    along_x = 0.25 * (padded[:, :, :-2] + 2.0 * padded[:, :, 1:-1] + padded[:, :, 2:])
    return 0.25 * (along_x[..., :-2] + 2.0 * along_x[..., 1:-1] + along_x[..., 2:])


def apply_inverse(hessian, vectors):
    diag_p = hessian[0]
    diag_s = hessian[1]
    diag_r = hessian[2]
    cross_ps = hessian[3]
    cross_pr = hessian[4]
    cross_sr = hessian[5]
    cof_pp = diag_s * diag_r - cross_sr * cross_sr
    cof_ps = cross_pr * cross_sr - cross_ps * diag_r
    cof_pr = cross_ps * cross_sr - diag_s * cross_pr
    cof_ss = diag_p * diag_r - cross_pr * cross_pr
    cof_sr = cross_ps * cross_pr - diag_p * cross_sr
    cof_rr = diag_p * diag_s - cross_ps * cross_ps
    determinant = diag_p * cof_pp + cross_ps * cof_ps + cross_pr * cof_pr
    inverse_det = 1.0 / determinant
    comp_one = vectors[:, 0]
    comp_two = vectors[:, 1]
    comp_three = vectors[:, 2]
    return jnp.stack(
        [
            (cof_pp * comp_one + cof_ps * comp_two + cof_pr * comp_three) * inverse_det,
            (cof_ps * comp_one + cof_ss * comp_two + cof_sr * comp_three) * inverse_det,
            (cof_pr * comp_one + cof_sr * comp_two + cof_rr * comp_three) * inverse_det,
        ],
        axis=1,
    )


def pair_dots(left_flat, right_flat):
    return lax.dot_general(
        left_flat,
        right_flat,
        (((1,), (1,)), ((), ())),
        precision=lax.Precision.HIGHEST,
        preferred_element_type=jnp.float32,
    )


def upper_solve(matrix, values):
    count = matrix.shape[0]
    found = [None] * count
    for row in range(count - 1, -1, -1):
        total = values[row]
        for col in range(row + 1, count):
            total = total - matrix[row, col] * found[col]
        found[row] = total / matrix[row, row]
    return jnp.stack(found)


def upper_transpose_solve(matrix, values):
    count = matrix.shape[0]
    found = [None] * count
    for row in range(count):
        total = values[row]
        for col in range(row):
            total = total - matrix[col, row] * found[col]
        found[row] = total / matrix[row, row]
    return jnp.stack(found)


def combine_terms(cross_gram, curv_gram, hist_dot, pre_dot, solved, hist_s):
    middle_part = jnp.diag(jnp.diag(cross_gram)) + curv_gram
    coef_p = upper_solve(cross_gram, hist_dot)
    right_hand = jnp.dot(middle_part, coef_p, precision=lax.Precision.HIGHEST) - pre_dot
    coef_q = upper_transpose_solve(cross_gram, right_hand)
    update_s = jnp.tensordot(coef_q, hist_s, axes=1, precision=lax.Precision.HIGHEST)
    update_z = jnp.tensordot(coef_p, solved[1:], axes=1, precision=lax.Precision.HIGHEST)
    return -(solved[0] + update_s - update_z)


def plain_device(partials, hist_s, hist_y):
    s_flat = hist_s.reshape(PAIRS, -1)
    y_flat = hist_y.reshape(PAIRS, -1)
    inverse_count = 1.0 / lax.axis_size("shot")
    level_sums = lax.psum_scatter(partials[0], "shot", scatter_dimension=1, tiled=True)
    fields = level_sums * inverse_count
    extended = extended_2(fields, (("gx", 2), ("gy", 3)), 1)
    smoothed = smooth_block(extended)
    gradient = smoothed[0:3]
    solved = apply_inverse(smoothed[3:9], jnp.concatenate([gradient[None], hist_y], axis=0))
    z_flat = solved[1:].reshape(PAIRS, -1)
    curv_part = pair_dots(y_flat, z_flat)
    hist_part = pair_dots(s_flat, gradient.reshape(1, -1))[:, 0]
    pre_part = pair_dots(y_flat, solved[0].reshape(1, -1))[:, 0]
    cross_gram, curv_gram, hist_dot, pre_dot = lax.psum(
        (pair_dots(s_flat, y_flat), curv_part, hist_part, pre_part), ("shot", "gx", "gy")
    )
    return combine_terms(cross_gram, curv_gram, hist_dot, pre_dot, solved, hist_s)


def mesh_fits(sizes):
    n_shot, n_x, n_y = sizes
    twos = n_shot & (n_shot - 1) == 0 and n_x & (n_x - 1) == 0
    return twos and n_shot <= 8 and n_x in (2, 4, 8) and n_y == 2


def per_device(partials, hist_s, hist_y):
    rows, width = hist_s.shape[3:]
    fits = mesh_fits([lax.axis_size(a) for a in AXES]) and rows == 8 and width == 4 * BLOCK
    return (exchanged if fits else plain_device)(partials, hist_s, hist_y)


def solution(mesh):
    return jax.shard_map(
        per_device,
        mesh=mesh,
        in_specs=(
            P("shot", None, None, "gx", "gy"),
            P(None, None, "shot", "gx", "gy"),
            P(None, None, "shot", "gx", "gy"),
        ),
        out_specs=P(None, "shot", "gx", "gy"),
        check_vma=False,
    )
```
